256 devices in a mesh: section: 2 (over core), expert: 32 (over y, z), mp: 4 (over x).
Axes of the slice: x: 4, y: 4, z: 8, core: 2. Of those that a mesh axis runs over, the one named last changes fastest.
Arguments:
- layer_inputs: bfloat16 [2, 8192, 2048], P('section', ('expert', 'mp')), may hold values from -6 to 6
- norm_gain: float32 [2, 2048], P('section'), may hold values from 0.1 to 1.9
- w_gate: bfloat16 [2, 64, 768, 2048], P('section', 'expert', 'mp'), may hold values from -0.125 to 0.125
- w_up: bfloat16 [2, 64, 768, 2048], P('section', 'expert', 'mp'), may hold values from -0.125 to 0.125
- w_down: bfloat16 [2, 64, 768, 2048], P('section', 'expert', 'mp'), may hold values from -0.21875 to 0.21875
- routes: int32 [2, 8192, 8], P('section', ('expert', 'mp')), may hold values from 0 to 63, all different within a row; in each aligned block of 32 rows (0 to 31, 32 to 63, ..., all dimensions but the last counted through in order) at most 5 rows name the same one
- probs: float32 [2, 8192, 8], P('section', ('expert', 'mp')), may hold values from 0.05 to 0.3
- cotangent: bfloat16 [8192, 2048], P(('expert', 'mp')), may hold values from -6 to 6
- sampled: int32 [1], replicated, may hold values from 0 to 1
Outputs:
- input_grads: bfloat16 [2, 8192, 2048], P('section', ('expert', 'mp'))
- gate_grads: float32 [2, 64, 768, 2048], P('section', 'expert', 'mp')
- up_grads: float32 [2, 64, 768, 2048], P('section', 'expert', 'mp')
The draws below stay inside these ranges and needn't reach their ends.
Inputs may be any that keep to these rules, and one draw needn't show every extreme that they name: `routes`: each row names 8 different experts and every expert is named somewhere. In each aligned block of 32 rows of a layer, no expert is named by more than 5 rows, and in some blocks one expert is named by exactly 5.
All inputs are finite; a program needn't handle non-finite values.
Results may differ from the reference program's by a relative error of at most 0.012.
Values may be sent and summed in bfloat16 or wider, within the bound.
No kernel may reach another device: no remote copies, remote signals or barrier semaphores. Data moves between devices by JAX's collectives and lax.ppermute only.
A program may use at most 192 MiB of HBM per device.

```python
import math
import jax
import jax.numpy as jnp
import numpy as np
from jax import lax

D = 2048
FF = 768
TOP = 8
EXPERTS = 64
TOK_DEV = 64
CAPH = 5
TOKENS = 8192
N_EXPERT = 32
N_MP = 4


def steps_of(key, extent, shards, smallest, largest):
    level, own = 1.0, jax.random.fold_in(key, 6)
    for position, blocks in shards:
        steps = jnp.exp(jax.random.uniform(jax.random.fold_in(own, position), (blocks,), jnp.float32, smallest / len(shards), largest / len(shards)))
        level = level * jnp.repeat(steps, extent[position] // blocks).reshape([-1 if axis == position else 1 for axis in range(len(extent))])
    return level


def shared_out(own_key, own, number, rows, count, top, most, slope):
    sequence = jax.random.permutation(own_key, count)
    crowded, ordinary = load_shares(count, rows * top, most, slope, True), load_shares(count, rows * top, most, slope, False)
    places = jnp.arange(count)

    def named(tallies, rotation):
        used = int((tallies > 0).sum())
        fixed = max(1, used // 4)
        moved = fixed + (places - fixed + rotation * (used - fixed)) % max(1, count - fixed)
        return jnp.zeros((count,), jnp.int32).at[sequence[jnp.where(places < fixed, places, moved)]].set(jnp.asarray(tallies, jnp.int32))

    tallies = jnp.where(number % 4 == 0, named(crowded, number // 4), named(ordinary, number - number // 4 - 1))
    mixed = jax.random.permutation(jax.random.fold_in(own, 3), count)
    donor, receiver = mixed[0:count // 2 * 2:2], mixed[1:count // 2 * 2:2]
    room = jnp.minimum(tallies[donor] - 1, most - tallies[receiver]) // 2
    room = jnp.where((donor == sequence[0]) | (receiver == sequence[0]) | (tallies[receiver] == 0), 0, jnp.maximum(room, 0))
    moved = jax.random.randint(jax.random.fold_in(own, 4), (count // 2,), 0, 1 << 20) % (room + 1)
    tallies = tallies.at[donor].add(-moved).at[receiver].add(moved)
    members = jnp.searchsorted(jnp.cumsum(tallies), jnp.arange(rows * top), side="right").astype(jnp.int32)
    table = members.reshape(top, rows).T
    table = table[jax.random.permutation(jax.random.fold_in(own, 1), rows)]
    rotation = jax.random.randint(jax.random.fold_in(own, 2), (rows, 1), 0, top)
    return jnp.take_along_axis(table, (jnp.arange(top)[None, :] + rotation) % top, axis=1)


def load_shares(amount, total, most, skew, full):
    portions = [(1 << 20) // math.isqrt(grade ** skew) + 1 for grade in range(1, amount + 1)]
    largest = most if full else min(most, max(-(-total // amount), total * portions[0] // sum(portions)))
    least = 1 if total - largest >= amount - 1 else 0
    counts, surplus = [largest] + [least] * (amount - 1), total - largest - least * (amount - 1)
    while surplus > 0:
        free = [i for i in range(1, amount) if counts[i] < largest] or [i for i in range(1, amount) if counts[i] < most]
        mass, remaining = sum([portions[i] for i in free]), surplus
        for i in free:
            extra = min(most - counts[i], max(1, remaining * portions[i] // mass), surplus)
            counts[i] = counts[i] + extra
            surplus = surplus - extra
    return np.array(counts)


def normal_values(own_key, extent, width, reach, shards=(), kind=jnp.bfloat16):
    drawn = width * jax.random.normal(own_key, extent, jnp.float32)
    if shards:
        drawn = drawn * steps_of(own_key, extent, shards, -0.22, 0.18)
    return jnp.clip(drawn, -reach, reach).astype(kind)


def setup_inputs(seed: int = 0) -> dict:
    splits = jax.random.split(jax.random.key(seed), 10)
    layer_inputs = normal_values(splits[0], (2, TOKENS, D), 1.0, 6.0, ((0, 2), (1, 128)))
    norm_gain = jnp.clip(1.0 + 0.18 * jax.random.normal(splits[1], (2, D), jnp.float32), 0.1, 1.9)
    w_gate = normal_values(splits[2], (2, EXPERTS, FF, D), D ** -0.5, 0.125, ((0, 2), (1, 32), (2, 4)))
    w_up = normal_values(splits[3], (2, EXPERTS, FF, D), D ** -0.5, 0.125, ((0, 2), (1, 32), (2, 4)))
    w_down = normal_values(splits[4], (2, EXPERTS, FF, D), FF ** -0.5, 0.21875, ((0, 2), (1, 32), (2, 4)))
    routes_keys = jax.random.split(jax.random.fold_in(splits[5], 1), 2 * TOKENS // (TOK_DEV // 2))
    routes_turns = jax.random.permutation(jax.random.fold_in(splits[5], 3), 2 * TOKENS // (TOK_DEV // 2))
    routes = jax.vmap(lambda own, number: shared_out(jax.random.fold_in(splits[5], 2), own, number, TOK_DEV // 2, EXPERTS, TOP, CAPH, 2))(routes_keys, routes_turns).reshape((2, TOKENS, TOP))
    probs = jnp.clip(0.05 + 0.25 * jax.random.uniform(splits[6], (2, TOKENS, TOP), jnp.float32) ** steps_of(splits[6], (2, TOKENS, TOP), ((0, 2), (1, 128)), -0.2, 0.2), 0.05, 0.3)
    cotangent = normal_values(splits[7], (TOKENS, D), 1.0, 6.0, ((0, 128),))
    sampled = jax.random.randint(splits[8], (1,), 0, 2).astype(jnp.int32)
    return dict(layer_inputs=layer_inputs, norm_gain=norm_gain, w_gate=w_gate, w_up=w_up, w_down=w_down, routes=routes, probs=probs, cotangent=cotangent, sampled=sampled)


epsilon = 1e-06

def normalize(inputs, gain_vector):
    values = inputs.astype(jnp.float32)
    factor = lax.rsqrt(lax.optimization_barrier(jnp.mean(values * values, axis=1, keepdims=True)) + epsilon)
    normed = values * factor
    return (normed, factor, (normed * gain_vector[None, :]).astype(jnp.bfloat16))

def expert_terms(operands, training):
    hidden_rows, weighted_rows, gate_w, up_w, down_w = operands
    gate_act = jnp.dot(hidden_rows, gate_w.T, preferred_element_type=jnp.float32)
    lifted = jnp.dot(hidden_rows, up_w.T, preferred_element_type=jnp.float32)
    back = jnp.dot(weighted_rows, down_w.T, preferred_element_type=jnp.float32)
    logistic = jax.nn.sigmoid(gate_act)
    d_gate = (back * lifted * logistic * (1.0 + gate_act * (1.0 - logistic))).astype(jnp.bfloat16)
    d_up = (back * gate_act * logistic).astype(jnp.bfloat16)
    slot_grad = (jnp.dot(d_gate, gate_w, preferred_element_type=jnp.float32) + jnp.dot(d_up, up_w, preferred_element_type=jnp.float32)).astype(jnp.bfloat16)

    def compute_grads():
        return (jnp.dot(d_gate.T, hidden_rows, preferred_element_type=jnp.float32), jnp.dot(d_up.T, hidden_rows, preferred_element_type=jnp.float32))

    def zero_grads():
        return (jnp.zeros((FF, D), jnp.float32), jnp.zeros((FF, D), jnp.float32))
    grad_gate, grad_up = lax.cond(training, compute_grads, zero_grads)
    return (slot_grad, grad_gate, grad_up)

def group_backward(inputs, gain_vector, gate_w, up_w, down_w, group_routes, group_probs, upstream, training):
    normed, factor, hidden = normalize(inputs, gain_vector)
    token_count = inputs.shape[0]
    limit = token_count // (TOK_DEV // 2) * CAPH
    flat_routes = group_routes.reshape(-1).astype(jnp.int32)
    onehot = (flat_routes[:, None] == jnp.arange(EXPERTS, dtype=jnp.int32)[None, :]).astype(jnp.int32)
    earlier = jnp.cumsum(onehot, axis=0) - onehot
    places = lax.optimization_barrier(jnp.sum(earlier * onehot, axis=1)).astype(jnp.int32)
    targets = (flat_routes * limit + places).astype(jnp.int32)
    hidden_slots = jnp.repeat(hidden, TOP, axis=0)
    weighted = (group_probs[:, :, None] * upstream[:, None, :].astype(jnp.float32)).astype(jnp.bfloat16)
    weighted = weighted.reshape(token_count * TOP, D)
    hidden_buffer = jnp.zeros((EXPERTS * limit, D), jnp.bfloat16).at[targets].set(hidden_slots).reshape(EXPERTS, limit, D)
    weighted_buffer = jnp.zeros((EXPERTS * limit, D), jnp.bfloat16).at[targets].set(weighted).reshape(EXPERTS, limit, D)
    slot_grads, grad_gate, grad_up = lax.map(lambda operands: expert_terms(operands, training), (hidden_buffer, weighted_buffer, gate_w, up_w, down_w))
    slot_values = slot_grads.reshape(EXPERTS * limit, D)[targets]
    token_grad = lax.optimization_barrier(jnp.sum(slot_values.reshape(token_count, TOP, D).astype(jnp.float32), axis=1))
    scaled = token_grad * gain_vector[None, :]
    inner = lax.optimization_barrier(jnp.mean(scaled * normed, axis=1, keepdims=True))
    input_grad = (upstream.astype(jnp.float32) + factor * (scaled - normed * inner)).astype(jnp.bfloat16)
    return (input_grad, grad_gate, grad_up)

def layer_backward(inputs, gain_vector, gate_w, up_w, down_w, layer_routes, layer_probs, upstream, training):

    def select(array, group):
        shaped = array.reshape((N_EXPERT, N_MP, TOK_DEV) + array.shape[1:])
        return shaped[:, group].reshape((N_EXPERT * TOK_DEV,) + array.shape[1:])
    grads_list = []
    gate_total = jnp.zeros((EXPERTS, FF, D), jnp.float32)
    up_total = jnp.zeros((EXPERTS, FF, D), jnp.float32)
    for group in range(N_MP):
        group_grad, group_gate, group_up = group_backward(select(inputs, group), gain_vector, gate_w, up_w, down_w, select(layer_routes, group), select(layer_probs, group), select(upstream, group), training)
        grads_list.append(group_grad.reshape(N_EXPERT, TOK_DEV, D))
        gate_total = gate_total + lax.optimization_barrier(group_gate.astype(jnp.bfloat16)).astype(jnp.float32)
        up_total = up_total + lax.optimization_barrier(group_up.astype(jnp.bfloat16)).astype(jnp.float32)
    input_grad = jnp.stack(grads_list, axis=1).reshape(N_EXPERT * N_MP * TOK_DEV, D)
    return (input_grad, gate_total, up_total)

def reference(layer_inputs, norm_gain, w_gate, w_up, w_down, routes, probs, cotangent, sampled):
    upper_grad, upper_gate, upper_up = layer_backward(layer_inputs[1], norm_gain[1], w_gate[1], w_up[1], w_down[1], routes[1], probs[1], cotangent, sampled[0] == 1)
    lower_grad, lower_gate, lower_up = layer_backward(layer_inputs[0], norm_gain[0], w_gate[0], w_up[0], w_down[0], routes[0], probs[0], upper_grad, sampled[0] == 0)
    return (jnp.stack([lower_grad, upper_grad]), jnp.stack([lower_gate, upper_gate]), jnp.stack([lower_up, upper_up]))
```

```python
import jax
import jax.numpy as jnp
from jax import lax
from jax.sharding import PartitionSpec as P


CAPH = 5
CAP = 2 * CAPH
LANES = 128


epsilon = 1e-06


def other_core(value):
    return lax.ppermute(value, "section", [(0, 1), (1, 0)])


def after(value, *earlier):
    return lax.optimization_barrier((value, *earlier))[0]


def turned(value, by):
    peers = lax.axis_size("mp")
    return lax.ppermute(value, "mp", [(i, (i + by) % peers) for i in range(peers)])


def ring_first(own):
    return turned(own, 1), turned(own, -1)


def ring_second(before, behind):
    half = before.shape[-2] // 2
    return (
        turned(before[..., :half, :], 1),
        turned(behind[..., half:, :], -1),
    )


def normalize(inputs, gain_vector):
    values = inputs.astype(jnp.float32)
    factor = lax.rsqrt(jnp.mean(values * values, axis=1, keepdims=True) + epsilon)
    normed = values * factor
    return (normed, factor, (normed * gain_vector[None, :]).astype(jnp.bfloat16))


def plan(token_routes, token_probs, experts_here):
    match = token_routes[:, :, None] == experts_here[None, None, :]
    named = jnp.any(match, axis=1)
    chance = jnp.sum(jnp.where(match, token_probs[:, :, None], 0.0), axis=1)
    tokens = token_routes.shape[0]
    earlier = (
        jnp.arange(tokens, dtype=jnp.int32)[:, None] > jnp.arange(tokens, dtype=jnp.int32)[None, :]
    )
    places = jnp.dot(
        earlier.astype(jnp.bfloat16),
        named.astype(jnp.bfloat16),
        preferred_element_type=jnp.float32,
    ).astype(jnp.int32)
    places = jnp.where(named, places, -1).T
    pick = places[:, None, :] == jnp.arange(CAP, dtype=jnp.int32)[None, :, None]
    row_prob = jnp.sum(jnp.where(pick, chance.T[:, None, :], 0.0), axis=2)
    return pick, row_prob


def to_wire(rows, peers):
    return rows.reshape(peers, rows.shape[0] // peers, rows.shape[1] // LANES, LANES)


def from_wire(wire):
    return wire.reshape(wire.shape[0] * wire.shape[1], wire.shape[2] * wire.shape[3])


def exchange(rows, peers):
    wire = to_wire(rows, peers)
    return from_wire(lax.all_to_all(wire, "expert", split_axis=0, concat_axis=0, tiled=True))


def over_rows(weights, rows):
    return lax.dot_general(
        weights, rows, (((1,), (1,)), ((), ())), preferred_element_type=jnp.float32
    )


def back_rows(weights, units):
    return lax.dot_general(
        units, weights, (((0,), (0,)), ((), ())), preferred_element_type=jnp.float32
    )


def expert_pass(hidden_rows, weighted_rows, gate_w, up_w, down_w):
    gate_act = over_rows(gate_w, hidden_rows)
    lifted = over_rows(up_w, hidden_rows)
    back = over_rows(down_w, weighted_rows)
    logistic = jax.nn.sigmoid(gate_act)
    d_gate = (back * lifted * logistic * (1.0 + gate_act * (1.0 - logistic))).astype(jnp.bfloat16)
    d_up = (back * gate_act * logistic).astype(jnp.bfloat16)
    slot_grad = (back_rows(gate_w, d_gate) + back_rows(up_w, d_up)).astype(jnp.bfloat16)
    return (slot_grad, d_gate, d_up)


def per_device(layer_inputs, norm_gain, w_gate, w_up, w_down, routes, probs, cotangent, sampled):
    section = lax.axis_index("section")
    upper = section == 1
    peers = lax.axis_size("expert")
    groups = lax.axis_size("mp")
    tokens, width = cotangent.shape
    top_count = routes.shape[2]

    def by_layer(own, peer):
        return (jnp.where(upper, peer, own), jnp.where(upper, own, peer))

    def split_experts(weights):
        keep = lax.dynamic_index_in_dim(weights[0], section, 0, keepdims=False)
        send = lax.dynamic_index_in_dim(weights[0], 1 - section, 0, keepdims=False)
        return by_layer(keep, other_core(send))

    gate_parts = split_experts(w_gate)
    up_parts = split_experts(w_up)
    down_parts = split_experts(w_down)
    own1 = jnp.stack([gate_parts[1], up_parts[1], down_parts[1]])
    own0 = jnp.stack([gate_parts[0], up_parts[0], down_parts[0]])
    before1, behind1 = ring_first(own1)
    small = jnp.concatenate(
        [norm_gain[0], routes[0].astype(jnp.float32).reshape(-1), probs[0].reshape(-1)]
    )
    small = after(small, own1)
    own_inputs = after(layer_inputs[0], own1)
    small_parts = by_layer(small, other_core(small))
    input_parts = by_layer(own_inputs, other_core(own_inputs))
    far1 = ring_second(before1, behind1)
    before0, behind0 = ring_first(after(own0, *far1))
    far0 = ring_second(before0, behind0)
    weights1 = jnp.concatenate([own1, before1, behind1, *far1], axis=1)
    weights0 = jnp.concatenate([own0, before0, behind0, *far0], axis=1)

    experts_here = 2 * jnp.arange(peers, dtype=jnp.int32) + section
    layers = []
    for layer in range(2):
        vector = small_parts[layer]
        gain_vector = vector[:width]
        token_routes = (
            vector[width : width + tokens * top_count].reshape(tokens, top_count).astype(jnp.int32)
        )
        token_probs = vector[width + tokens * top_count :].reshape(tokens, top_count)
        normed, factor, hidden = normalize(input_parts[layer], gain_vector)
        pick, row_prob = plan(token_routes, token_probs, experts_here)
        layers.append((gain_vector, normed, factor, hidden, pick, row_prob))

    def spread(pick, rows):
        flat = pick.astype(jnp.bfloat16).reshape(-1, pick.shape[2])
        return jnp.dot(flat, rows, preferred_element_type=jnp.float32)

    pick1, pick0 = layers[1][4], layers[0][4]

    def scaled_rows(pick, row_prob, upstream):
        rows = spread(pick, upstream) * row_prob.reshape(-1, 1)
        return rows.astype(jnp.bfloat16)

    first = jnp.concatenate(
        [
            to_wire(spread(pick1, layers[1][3]).astype(jnp.bfloat16), peers),
            to_wire(scaled_rows(pick1, layers[1][5], cotangent), peers),
        ],
        axis=1,
    )
    arrived = lax.all_to_all(first, "expert", split_axis=0, concat_axis=0, tiled=True)
    hidden1 = from_wire(arrived[:, :CAP])
    weighted1 = from_wire(arrived[:, CAP:])
    second = to_wire(spread(pick0, layers[0][3]).astype(jnp.bfloat16), peers)
    hidden0 = from_wire(lax.all_to_all(second, "expert", split_axis=0, concat_axis=0, tiled=True))
    trained1 = sampled[0] == 1

    def finish(layer, sent, upstream):
        gain_vector, normed, factor, _, pick, _ = layers[layer]
        returned = from_wire(
            lax.all_to_all(sent, "expert", split_axis=0, concat_axis=0, tiled=True)
        )
        flat = pick.astype(jnp.bfloat16).reshape(-1, tokens)
        partial = lax.dot_general(
            flat, returned, (((0,), (0,)), ((), ())), preferred_element_type=jnp.float32
        )
        token_grad = partial + other_core(partial)
        scaled = token_grad * gain_vector[None, :]
        inner = jnp.mean(scaled * normed, axis=1, keepdims=True)
        return (upstream.astype(jnp.float32) + factor * (scaled - normed * inner)).astype(
            jnp.bfloat16
        )

    slot_grad1, d_gate1, d_up1 = expert_pass(hidden1, weighted1, weights1[0], weights1[1], weights1[2])
    trained_hidden = jnp.where(trained1, *after((hidden1, hidden0), slot_grad1))
    before_h, behind_h = ring_first(after(trained_hidden, *far0))
    far_h = ring_second(before_h, behind_h)
    far_h = jnp.concatenate(far_h, axis=0)
    input_grad1 = finish(1, to_wire(slot_grad1, peers), cotangent)
    weighted0 = exchange(
        scaled_rows(pick0, layers[0][5], input_grad1), peers
    )
    slot_grad0, d_gate0, d_up0 = expert_pass(hidden0, weighted0, weights0[0], weights0[1], weights0[2])
    sent0 = to_wire(slot_grad0, peers)
    input_grad0 = finish(0, sent0, input_grad1)
    result = jnp.where(upper, input_grad1, input_grad0)

    units = d_gate1.shape[0] // groups
    d_gate = jnp.where(trained1, d_gate1, d_gate0).reshape(groups, units, -1)
    d_up = jnp.where(trained1, d_up1, d_up0).reshape(groups, units, -1)
    d_both = after(jnp.concatenate([d_gate, d_up], axis=1), sent0)
    d_behind = turned(d_both[1], -1)
    d_before = turned(d_both[2], 1)
    d_far = turned(d_both[3], 2)
    grads = jnp.dot(d_both[0], trained_hidden, preferred_element_type=jnp.float32)
    grads = grads + jnp.dot(d_before, before_h, preferred_element_type=jnp.float32)
    grads = grads + jnp.dot(d_behind, behind_h, preferred_element_type=jnp.float32)
    grads = grads + jnp.dot(d_far, far_h, preferred_element_type=jnp.float32)
    grads = grads.astype(jnp.bfloat16)
    from_other = other_core(grads)
    trained = sampled[0] == section
    pair = jnp.stack(
        [jnp.where(upper, from_other, grads), jnp.where(upper, grads, from_other)], axis=0
    )
    pair = jnp.where(trained, pair.astype(jnp.float32), 0.0)
    return (result[None], pair[None, :, :units], pair[None, :, units:])


def solution(mesh):
    placed = (
        P("section", ("expert", "mp"), None),
        P("section", None),
        P("section", "expert", "mp", None),
        P("section", "expert", "mp", None),
        P("section", "expert", "mp", None),
        P("section", ("expert", "mp"), None),
        P("section", ("expert", "mp"), None),
        P(("expert", "mp"), None),
        P(),
    )
    return jax.shard_map(
        per_device,
        mesh=mesh,
        in_specs=placed,
        out_specs=(
            P("section", ("expert", "mp"), None),
            P("section", "expert", "mp", None),
            P("section", "expert", "mp", None),
        ),
        check_vma=False,
    )
```

```python
import jax
import jax.numpy as jnp
from jax import lax
from jax.sharding import PartitionSpec as P


CAPH = 5
CAP = 2 * CAPH
LANES = 128


epsilon = 1e-06


def other_core(value):
    return lax.ppermute(value, "section", [(0, 1), (1, 0)])


def after(value, *earlier):
    return lax.optimization_barrier((value, *earlier))[0]


def turned(value, by):
    peers = lax.axis_size("mp")
    return lax.ppermute(value, "mp", [(i, (i + by) % peers) for i in range(peers)])


def ring_first(own):
    return turned(own, 1), turned(own, -1)


def ring_second(before, behind):
    half = before.shape[-2] // 2
    return (
        turned(before[..., :half, :], 1),
        turned(behind[..., half:, :], -1),
    )


def normalize(inputs, gain_vector):
    values = inputs.astype(jnp.float32)
    factor = lax.rsqrt(jnp.mean(values * values, axis=1, keepdims=True) + epsilon)
    normed = values * factor
    return (normed, factor, (normed * gain_vector[None, :]).astype(jnp.bfloat16))


def plan(token_routes, token_probs, experts_here):
    match = token_routes[:, :, None] == experts_here[None, None, :]
    named = jnp.any(match, axis=1)
    chance = jnp.sum(jnp.where(match, token_probs[:, :, None], 0.0), axis=1)
    tokens = token_routes.shape[0]
    earlier = (
        jnp.arange(tokens, dtype=jnp.int32)[:, None] > jnp.arange(tokens, dtype=jnp.int32)[None, :]
    )
    places = jnp.dot(
        earlier.astype(jnp.bfloat16),
        named.astype(jnp.bfloat16),
        preferred_element_type=jnp.float32,
    ).astype(jnp.int32)
    places = jnp.where(named, places, -1).T
    pick = places[:, None, :] == jnp.arange(CAP, dtype=jnp.int32)[None, :, None]
    row_prob = jnp.sum(jnp.where(pick, chance.T[:, None, :], 0.0), axis=2)
    return pick, row_prob


def to_wire(rows, peers):
    return rows.reshape(peers, rows.shape[0] // peers, rows.shape[1] // LANES, LANES)


def from_wire(wire):
    return wire.reshape(wire.shape[0] * wire.shape[1], wire.shape[2] * wire.shape[3])


def exchange(rows, peers):
    wire = to_wire(rows, peers)
    return from_wire(lax.all_to_all(wire, "expert", split_axis=0, concat_axis=0, tiled=True))


def over_rows(weights, rows):
    return lax.dot_general(
        weights, rows, (((1,), (1,)), ((), ())), preferred_element_type=jnp.float32
    )


def back_rows(weights, units):
    return lax.dot_general(
        units, weights, (((0,), (0,)), ((), ())), preferred_element_type=jnp.float32
    )


def expert_pass(hidden_rows, weighted_rows, gate_w, up_w, down_w):
    gate_act = over_rows(gate_w, hidden_rows)
    lifted = over_rows(up_w, hidden_rows)
    back = over_rows(down_w, weighted_rows)
    logistic = jax.nn.sigmoid(gate_act)
    d_gate = (back * lifted * logistic * (1.0 + gate_act * (1.0 - logistic))).astype(jnp.bfloat16)
    d_up = (back * gate_act * logistic).astype(jnp.bfloat16)
    slot_grad = (back_rows(gate_w, d_gate) + back_rows(up_w, d_up)).astype(jnp.bfloat16)
    return (slot_grad, d_gate, d_up)


def per_device(layer_inputs, norm_gain, w_gate, w_up, w_down, routes, probs, cotangent, sampled):
    section = lax.axis_index("section")
    upper = section == 1
    peers = lax.axis_size("expert")
    groups = lax.axis_size("mp")
    tokens, width = cotangent.shape
    top_count = routes.shape[2]

    def both_layers(weights):
        return lax.all_to_all(weights[0], "section", split_axis=0, concat_axis=0, tiled=True)

    parts = [both_layers(weights) for weights in (w_gate, w_up, w_down)]
    own1 = jnp.stack([part[1] for part in parts])
    own0 = jnp.stack([part[0] for part in parts])
    before1, behind1 = ring_first(own1)
    small = jnp.concatenate(
        [norm_gain[0], routes[0].astype(jnp.float32).reshape(-1), probs[0].reshape(-1)]
    )
    small_parts = lax.all_gather(small, "section", axis=0)
    input_parts = lax.all_gather(layer_inputs[0], "section", axis=0)
    far1 = ring_second(before1, behind1)
    before0, behind0 = ring_first(after(own0, *far1))
    far0 = ring_second(before0, behind0)
    weights1 = jnp.concatenate([own1, before1, behind1, *far1], axis=1)
    weights0 = jnp.concatenate([own0, before0, behind0, *far0], axis=1)

    experts_here = 2 * jnp.arange(peers, dtype=jnp.int32) + section
    layers = []
    for layer in range(2):
        vector = small_parts[layer]
        gain_vector = vector[:width]
        token_routes = (
            vector[width : width + tokens * top_count].reshape(tokens, top_count).astype(jnp.int32)
        )
        token_probs = vector[width + tokens * top_count :].reshape(tokens, top_count)
        normed, factor, hidden = normalize(input_parts[layer], gain_vector)
        pick, row_prob = plan(token_routes, token_probs, experts_here)
        layers.append((gain_vector, normed, factor, hidden, pick, row_prob))

    def spread(pick, rows):
        flat = pick.astype(jnp.bfloat16).reshape(-1, pick.shape[2])
        return jnp.dot(flat, rows, preferred_element_type=jnp.float32)

    pick1, pick0 = layers[1][4], layers[0][4]

    def scaled_rows(pick, row_prob, upstream):
        rows = spread(pick, upstream) * row_prob.reshape(-1, 1)
        return rows.astype(jnp.bfloat16)

    first = jnp.concatenate(
        [
            to_wire(spread(pick1, layers[1][3]).astype(jnp.bfloat16), peers),
            to_wire(scaled_rows(pick1, layers[1][5], cotangent), peers),
        ],
        axis=1,
    )
    arrived = lax.all_to_all(first, "expert", split_axis=0, concat_axis=0, tiled=True)
    hidden1 = from_wire(arrived[:, :CAP])
    weighted1 = from_wire(arrived[:, CAP:])
    second = to_wire(spread(pick0, layers[0][3]).astype(jnp.bfloat16), peers)
    hidden0 = from_wire(lax.all_to_all(second, "expert", split_axis=0, concat_axis=0, tiled=True))
    trained1 = sampled[0] == 1

    def finish(layer, sent, upstream):
        gain_vector, normed, factor, _, pick, _ = layers[layer]
        returned = from_wire(
            lax.all_to_all(sent, "expert", split_axis=0, concat_axis=0, tiled=True)
        )
        flat = pick.astype(jnp.bfloat16).reshape(-1, tokens)
        partial = lax.dot_general(
            flat, returned, (((0,), (0,)), ((), ())), preferred_element_type=jnp.float32
        )
        token_grad = partial + other_core(partial)
        scaled = token_grad * gain_vector[None, :]
        inner = jnp.mean(scaled * normed, axis=1, keepdims=True)
        return (upstream.astype(jnp.float32) + factor * (scaled - normed * inner)).astype(
            jnp.bfloat16
        )

    slot_grad1, d_gate1, d_up1 = expert_pass(hidden1, weighted1, weights1[0], weights1[1], weights1[2])
    trained_hidden = jnp.where(trained1, *after((hidden1, hidden0), slot_grad1))
    before_h, behind_h = ring_first(after(trained_hidden, *far0))
    far_h = ring_second(before_h, behind_h)
    far_h = jnp.concatenate(far_h, axis=0)
    input_grad1 = finish(1, to_wire(slot_grad1, peers), cotangent)
    weighted0 = exchange(scaled_rows(pick0, layers[0][5], input_grad1), peers)
    slot_grad0, d_gate0, d_up0 = expert_pass(hidden0, weighted0, weights0[0], weights0[1], weights0[2])
    sent0 = to_wire(slot_grad0, peers)
    input_grad0 = finish(0, sent0, input_grad1)
    result = jnp.where(upper, input_grad1, input_grad0)

    units = d_gate1.shape[0] // groups
    d_gate = jnp.where(trained1, d_gate1, d_gate0).reshape(groups, units, -1)
    d_up = jnp.where(trained1, d_up1, d_up0).reshape(groups, units, -1)
    d_both = after(jnp.concatenate([d_gate, d_up], axis=1), sent0)
    d_behind = turned(d_both[1], -1)
    d_before = turned(d_both[2], 1)
    d_far = turned(d_both[3], 2)
    grads = jnp.dot(d_both[0], trained_hidden, preferred_element_type=jnp.float32)
    grads = grads + jnp.dot(d_before, before_h, preferred_element_type=jnp.float32)
    grads = grads + jnp.dot(d_behind, behind_h, preferred_element_type=jnp.float32)
    grads = grads + jnp.dot(d_far, far_h, preferred_element_type=jnp.float32)
    trained = sampled[0] == section

    def on_owner(part):
        twice = jnp.broadcast_to(part.astype(jnp.bfloat16)[None], (2,) + part.shape)
        pair = lax.all_to_all(twice, "section", split_axis=0, concat_axis=0, tiled=True)
        return jnp.where(trained, pair.astype(jnp.float32), 0.0)[None]

    return (result[None], on_owner(grads[:units]), on_owner(grads[units:]))


def solution(mesh):
    placed = (
        P("section", ("expert", "mp"), None),
        P("section", None),
        P("section", "expert", "mp", None),
        P("section", "expert", "mp", None),
        P("section", "expert", "mp", None),
        P("section", ("expert", "mp"), None),
        P("section", ("expert", "mp"), None),
        P(("expert", "mp"), None),
        P(),
    )
    return jax.shard_map(
        per_device,
        mesh=mesh,
        in_specs=placed,
        out_specs=(
            P("section", ("expert", "mp"), None),
            P("section", "expert", "mp", None),
            P("section", "expert", "mp", None),
        ),
        check_vma=False,
    )
```

```python
import functools

import jax
import jax.numpy as jnp
from jax import lax
from jax.experimental import pallas as pl
from jax.experimental.pallas import tpu as pltpu
from jax.sharding import PartitionSpec as P


CAPH = 5
CAP = 2 * CAPH
LANES = 128


epsilon = 1e-06


def other_core(value):
    return lax.ppermute(value, "section", [(0, 1), (1, 0)])


def after(value, *earlier):
    return lax.optimization_barrier((value, *earlier))[0]


def turned(value, by):
    peers = lax.axis_size("mp")
    return lax.ppermute(value, "mp", [(i, (i + by) % peers) for i in range(peers)])


def ring_first(own):
    return turned(own, 1), turned(own, -1)


def ring_second(before, behind):
    half = before.shape[-2] // 2
    return (
        turned(before[..., :half, :], 1),
        turned(behind[..., half:, :], -1),
    )


def pick_kernel(index_ref, gate_ref, up_ref, down_ref, out_ref):
    out_ref[0] = gate_ref[0]
    out_ref[1] = up_ref[0]
    out_ref[2] = down_ref[0]


def expert_part(index, weights, blocks):
    _, units, width = weights[0].shape
    rows = units // blocks
    spec = pl.BlockSpec((1, rows, width), lambda i, index_ref: (index_ref[0], i, 0))
    return pl.pallas_call(
        pick_kernel,
        grid_spec=pltpu.PrefetchScalarGridSpec(
            num_scalar_prefetch=1,
            grid=(blocks,),
            in_specs=[spec] * 3,
            out_specs=pl.BlockSpec((3, rows, width), lambda i, index_ref: (0, i, 0)),
        ),
        out_shape=jax.ShapeDtypeStruct((3, units, width), weights[0].dtype),
        name="expert_part",
    )(index, *weights)


def choose_kernel(keep, index_ref, got_ref, gate_ref, up_ref, down_ref, out_ref):
    @pl.when(index_ref[0] == keep)
    def _():
        out_ref[0] = gate_ref[0]
        out_ref[1] = up_ref[0]
        out_ref[2] = down_ref[0]

    @pl.when(index_ref[0] != keep)
    def _():
        out_ref[...] = got_ref[...]


def layer_part(layer, first, count, blocks, index, got, weights):
    _, units, width = weights[0].shape
    rows = units // blocks
    own = pl.BlockSpec((1, rows, width), lambda i, index_ref: (index_ref[0], first + i, 0))
    return pl.pallas_call(
        functools.partial(choose_kernel, layer),
        grid_spec=pltpu.PrefetchScalarGridSpec(
            num_scalar_prefetch=1,
            grid=(count,),
            in_specs=[pl.BlockSpec((3, rows, width), lambda i, index_ref: (0, first + i, 0))]
            + [own] * 3,
            out_specs=pl.BlockSpec((3, rows, width), lambda i, index_ref: (0, i, 0)),
        ),
        out_shape=jax.ShapeDtypeStruct((3, count * rows, width), weights[0].dtype),
        name="layer_part",
    )(index, got, *weights)


def normalize(inputs, gain_vector):
    values = inputs.astype(jnp.float32)
    factor = lax.rsqrt(jnp.mean(values * values, axis=1, keepdims=True) + epsilon)
    normed = values * factor
    return (normed, factor, (normed * gain_vector[None, :]).astype(jnp.bfloat16))


def plan(token_routes, token_probs, experts_here):
    match = token_routes[:, :, None] == experts_here[None, None, :]
    named = jnp.any(match, axis=1)
    chance = jnp.sum(jnp.where(match, token_probs[:, :, None], 0.0), axis=1)
    tokens = token_routes.shape[0]
    earlier = (
        jnp.arange(tokens, dtype=jnp.int32)[:, None] > jnp.arange(tokens, dtype=jnp.int32)[None, :]
    )
    places = jnp.dot(
        earlier.astype(jnp.bfloat16),
        named.astype(jnp.bfloat16),
        preferred_element_type=jnp.float32,
    ).astype(jnp.int32)
    places = jnp.where(named, places, -1).T
    pick = places[:, None, :] == jnp.arange(CAP, dtype=jnp.int32)[None, :, None]
    row_prob = jnp.sum(jnp.where(pick, chance.T[:, None, :], 0.0), axis=2)
    return pick, row_prob


def to_wire(rows, peers):
    return rows.reshape(peers, rows.shape[0] // peers, rows.shape[1] // LANES, LANES)


def from_wire(wire):
    return wire.reshape(wire.shape[0] * wire.shape[1], wire.shape[2] * wire.shape[3])


def exchange(rows, peers):
    wire = to_wire(rows, peers)
    return from_wire(lax.all_to_all(wire, "expert", split_axis=0, concat_axis=0, tiled=True))


def over_rows(weights, rows):
    return lax.dot_general(
        weights, rows, (((1,), (1,)), ((), ())), preferred_element_type=jnp.float32
    )


def back_rows(weights, units):
    return lax.dot_general(
        units, weights, (((0,), (0,)), ((), ())), preferred_element_type=jnp.float32
    )


def expert_pass(hidden_rows, weighted_rows, gate_w, up_w, down_w):
    gate_act = over_rows(gate_w, hidden_rows)
    lifted = over_rows(up_w, hidden_rows)
    back = over_rows(down_w, weighted_rows)
    logistic = jax.nn.sigmoid(gate_act)
    d_gate = (back * lifted * logistic * (1.0 + gate_act * (1.0 - logistic))).astype(jnp.bfloat16)
    d_up = (back * gate_act * logistic).astype(jnp.bfloat16)
    slot_grad = (back_rows(gate_w, d_gate) + back_rows(up_w, d_up)).astype(jnp.bfloat16)
    return (slot_grad, d_gate, d_up)


def per_device(layer_inputs, norm_gain, w_gate, w_up, w_down, routes, probs, cotangent, sampled):
    section = lax.axis_index("section")
    upper = section == 1
    peers = lax.axis_size("expert")
    groups = lax.axis_size("mp")
    tokens, width = cotangent.shape
    top_count = routes.shape[2]

    stored = (w_gate[0], w_up[0], w_down[0])
    index = section.astype(jnp.int32).reshape(1)
    got = other_core(expert_part(1 - index, stored, 4))
    head1 = layer_part(1, 0, 2, 4, index, got, stored)
    tail1 = layer_part(1, 2, 2, 4, index, got, stored)
    head_before = turned(head1, 1)
    tail_behind = turned(tail1, -1)
    tail_before = turned(tail1, 1)
    head_behind = turned(head1, -1)
    head_far = turned(head_before, 1)
    tail_far = turned(tail_behind, -1)
    small = jnp.concatenate(
        [norm_gain[0], routes[0].astype(jnp.float32).reshape(-1), probs[0].reshape(-1)]
    )
    small = after(small, head1)
    own_inputs = after(layer_inputs[0], head1)
    small_parts = lax.all_gather(small, "section", axis=0)
    input_parts = lax.all_gather(own_inputs, "section", axis=0)
    own0 = layer_part(0, 0, 4, 4, index, after(got, tail1), stored)
    before0, behind0 = ring_first(after(own0, head_far, tail_far))
    far0 = turned(before0, 1)
    weights1 = jnp.concatenate(
        [head1, tail1, head_before, tail_before, head_behind, tail_behind, head_far, tail_far],
        axis=1,
    )
    weights0 = jnp.concatenate([own0, before0, behind0, far0], axis=1)

    experts_here = 2 * jnp.arange(peers, dtype=jnp.int32) + section
    layers = []
    for layer in range(2):
        vector = small_parts[layer]
        gain_vector = vector[:width]
        token_routes = (
            vector[width : width + tokens * top_count].reshape(tokens, top_count).astype(jnp.int32)
        )
        token_probs = vector[width + tokens * top_count :].reshape(tokens, top_count)
        normed, factor, hidden = normalize(input_parts[layer], gain_vector)
        pick, row_prob = plan(token_routes, token_probs, experts_here)
        layers.append((gain_vector, normed, factor, hidden, pick, row_prob))

    def spread(pick, rows):
        flat = pick.astype(jnp.bfloat16).reshape(-1, pick.shape[2])
        return jnp.dot(flat, rows, preferred_element_type=jnp.float32)

    pick1, pick0 = layers[1][4], layers[0][4]

    def scaled_rows(pick, row_prob, upstream):
        rows = spread(pick, upstream) * row_prob.reshape(-1, 1)
        return rows.astype(jnp.bfloat16)

    first = jnp.concatenate(
        [
            to_wire(spread(pick1, layers[1][3]).astype(jnp.bfloat16), peers),
            to_wire(scaled_rows(pick1, layers[1][5], cotangent), peers),
        ],
        axis=1,
    )
    arrived = lax.all_to_all(first, "expert", split_axis=0, concat_axis=0, tiled=True)
    hidden1 = from_wire(arrived[:, :CAP])
    weighted1 = from_wire(arrived[:, CAP:])
    second = to_wire(spread(pick0, layers[0][3]).astype(jnp.bfloat16), peers)
    hidden0 = from_wire(lax.all_to_all(second, "expert", split_axis=0, concat_axis=0, tiled=True))
    trained1 = sampled[0] == 1

    def finish(layer, sent, upstream):
        gain_vector, normed, factor, _, pick, _ = layers[layer]
        returned = from_wire(
            lax.all_to_all(sent, "expert", split_axis=0, concat_axis=0, tiled=True)
        )
        flat = pick.astype(jnp.bfloat16).reshape(-1, tokens)
        partial = lax.dot_general(
            flat, returned, (((0,), (0,)), ((), ())), preferred_element_type=jnp.float32
        )
        token_grad = partial + other_core(partial)
        scaled = token_grad * gain_vector[None, :]
        inner = jnp.mean(scaled * normed, axis=1, keepdims=True)
        return (upstream.astype(jnp.float32) + factor * (scaled - normed * inner)).astype(
            jnp.bfloat16
        )

    slot_grad1, d_gate1, d_up1 = expert_pass(hidden1, weighted1, weights1[0], weights1[1], weights1[2])
    trained_hidden = jnp.where(trained1, *after((hidden1, hidden0), slot_grad1))
    before_h, behind_h = ring_first(after(trained_hidden, far0))
    far_h = ring_second(before_h, behind_h)
    far_h = jnp.concatenate(far_h, axis=0)
    input_grad1 = finish(1, to_wire(slot_grad1, peers), cotangent)
    weighted0 = exchange(scaled_rows(pick0, layers[0][5], input_grad1), peers)
    slot_grad0, d_gate0, d_up0 = expert_pass(hidden0, weighted0, weights0[0], weights0[1], weights0[2])
    sent0 = to_wire(slot_grad0, peers)
    input_grad0 = finish(0, sent0, input_grad1)
    result = jnp.where(upper, input_grad1, input_grad0)

    units = d_gate1.shape[0] // groups
    d_gate = jnp.where(trained1, d_gate1, d_gate0).reshape(groups, units, -1)
    d_up = jnp.where(trained1, d_up1, d_up0).reshape(groups, units, -1)
    d_both = after(jnp.concatenate([d_gate, d_up], axis=1), sent0)
    d_behind = turned(d_both[1], -1)
    d_before = turned(d_both[2], 1)
    d_far = turned(d_both[3], 2)
    grads = jnp.dot(d_both[0], trained_hidden, preferred_element_type=jnp.float32)
    grads = grads + jnp.dot(d_before, before_h, preferred_element_type=jnp.float32)
    grads = grads + jnp.dot(d_behind, behind_h, preferred_element_type=jnp.float32)
    grads = grads + jnp.dot(d_far, far_h, preferred_element_type=jnp.float32)
    grads = grads.astype(jnp.bfloat16)
    from_other = other_core(grads)
    trained = sampled[0] == section

    def on_owner(mine, theirs):
        low = jnp.where(upper, theirs, mine)
        high = jnp.where(upper, mine, theirs)
        pair = jnp.stack([low, high]).astype(jnp.float32)
        return jnp.where(trained, pair, 0.0)[None]

    gate_share = on_owner(grads[:units], from_other[:units])
    up_share = on_owner(grads[units:], from_other[units:])
    return (result[None], gate_share, up_share)


def solution(mesh):
    placed = (
        P("section", ("expert", "mp"), None),
        P("section", None),
        P("section", "expert", "mp", None),
        P("section", "expert", "mp", None),
        P("section", "expert", "mp", None),
        P("section", ("expert", "mp"), None),
        P("section", ("expert", "mp"), None),
        P(("expert", "mp"), None),
        P(),
    )
    return jax.shard_map(
        per_device,
        mesh=mesh,
        in_specs=placed,
        out_specs=(
            P("section", ("expert", "mp"), None),
            P("section", "expert", "mp", None),
            P("section", "expert", "mp", None),
        ),
        check_vma=False,
    )
```

```python
import functools

import jax
import jax.numpy as jnp
from jax import lax
from jax.experimental import pallas as pl
from jax.experimental.pallas import tpu as pltpu
from jax.sharding import PartitionSpec as P


CAPH = 5
CAP = 2 * CAPH
LANES = 128


epsilon = 1e-06


def other_core(value):
    return lax.ppermute(value, "section", [(0, 1), (1, 0)])


def after(value, *earlier):
    return lax.optimization_barrier((value, *earlier))[0]


def turned(value, by):
    peers = lax.axis_size("mp")
    return lax.ppermute(value, "mp", [(i, (i + by) % peers) for i in range(peers)])


def ring_first(own):
    return turned(own, 1), turned(own, -1)


def ring_second(before, behind):
    half = before.shape[-2] // 2
    return (
        turned(before[..., :half, :], 1),
        turned(behind[..., half:, :], -1),
    )


def pick_kernel(index_ref, gate_ref, up_ref, down_ref, out_ref):
    out_ref[0] = gate_ref[0]
    out_ref[1] = up_ref[0]
    out_ref[2] = down_ref[0]


def expert_part(index, weights, blocks):
    _, units, width = weights[0].shape
    rows = units // blocks
    spec = pl.BlockSpec((1, rows, width), lambda i, index_ref: (index_ref[0], i, 0))
    return pl.pallas_call(
        pick_kernel,
        grid_spec=pltpu.PrefetchScalarGridSpec(
            num_scalar_prefetch=1,
            grid=(blocks,),
            in_specs=[spec] * 3,
            out_specs=pl.BlockSpec((3, rows, width), lambda i, index_ref: (0, i, 0)),
        ),
        out_shape=jax.ShapeDtypeStruct((3, units, width), weights[0].dtype),
        name="expert_part",
    )(index, *weights)


def choose_kernel(keep, index_ref, got_ref, gate_ref, up_ref, down_ref, out_ref):
    @pl.when(index_ref[0] == keep)
    def _():
        out_ref[0] = gate_ref[0]
        out_ref[1] = up_ref[0]
        out_ref[2] = down_ref[0]

    @pl.when(index_ref[0] != keep)
    def _():
        out_ref[...] = got_ref[...]


def layer_part(layer, first, count, blocks, index, got, weights):
    _, units, width = weights[0].shape
    rows = units // blocks
    own = pl.BlockSpec((1, rows, width), lambda i, index_ref: (index_ref[0], first + i, 0))
    return pl.pallas_call(
        functools.partial(choose_kernel, layer),
        grid_spec=pltpu.PrefetchScalarGridSpec(
            num_scalar_prefetch=1,
            grid=(count,),
            in_specs=[pl.BlockSpec((3, rows, width), lambda i, index_ref: (0, first + i, 0))]
            + [own] * 3,
            out_specs=pl.BlockSpec((3, rows, width), lambda i, index_ref: (0, i, 0)),
        ),
        out_shape=jax.ShapeDtypeStruct((3, count * rows, width), weights[0].dtype),
        name="layer_part",
    )(index, got, *weights)


def normalize(inputs, gain_vector):
    values = inputs.astype(jnp.float32)
    factor = lax.rsqrt(jnp.mean(values * values, axis=1, keepdims=True) + epsilon)
    normed = values * factor
    return (normed, factor, (normed * gain_vector[None, :]).astype(jnp.bfloat16))


def plan(token_routes, token_probs, experts_here):
    match = token_routes[:, :, None] == experts_here[None, None, :]
    named = jnp.any(match, axis=1)
    chance = jnp.sum(jnp.where(match, token_probs[:, :, None], 0.0), axis=1)
    tokens = token_routes.shape[0]
    earlier = (
        jnp.arange(tokens, dtype=jnp.int32)[:, None] > jnp.arange(tokens, dtype=jnp.int32)[None, :]
    )
    places = jnp.dot(
        earlier.astype(jnp.bfloat16),
        named.astype(jnp.bfloat16),
        preferred_element_type=jnp.float32,
    ).astype(jnp.int32)
    places = jnp.where(named, places, -1).T
    pick = places[:, None, :] == jnp.arange(CAP, dtype=jnp.int32)[None, :, None]
    row_prob = jnp.sum(jnp.where(pick, chance.T[:, None, :], 0.0), axis=2)
    return pick, row_prob


def to_wire(rows, peers):
    return rows.reshape(peers, rows.shape[0] // peers, rows.shape[1] // LANES, LANES)


def from_wire(wire):
    return wire.reshape(wire.shape[0] * wire.shape[1], wire.shape[2] * wire.shape[3])


def exchange(rows, peers):
    wire = to_wire(rows, peers)
    return from_wire(lax.all_to_all(wire, "expert", split_axis=0, concat_axis=0, tiled=True))


def back_rows(weights, rows):
    return lax.dot_general(
        weights, rows, (((0,), (0,)), ((), ())), preferred_element_type=jnp.float32
    )


def expert_kernel(pieces, hidden_ref, weighted_ref, *refs):
    weight_refs, (slot_ref, d_ref, held, sems) = refs[:pieces], refs[pieces:]
    parts, _, units, width = held.shape
    rows = weight_refs[0].shape[1]
    each = units // rows

    def place(part, number):
        return held.at[part, :, pl.ds(number * rows, rows), :]

    for number, ref in enumerate(weight_refs):
        part = number // each
        pltpu.make_async_copy(ref, place(part, number % each), sems.at[number]).start()

    def along(rows_ref, part, which):
        return lax.dot_general(
            rows_ref[...],
            held[part, which],
            (((1,), (1,)), ((), ())),
            preferred_element_type=jnp.float32,
        )

    def one_part(part, carry):
        for number in range(each):
            there = place(part, number)
            pltpu.make_async_copy(there, there, sems.at[part * each + number]).wait()
        gate_act = along(hidden_ref, part, 0)
        lifted = along(hidden_ref, part, 1)
        back = along(weighted_ref, part, 2)
        logistic = jax.nn.sigmoid(gate_act)
        d_gate = back * lifted * logistic * (1.0 + gate_act * (1.0 - logistic))
        d_up = back * gate_act * logistic
        d_ref[part] = jnp.concatenate([d_gate, d_up], axis=1).astype(jnp.bfloat16)
        return carry

    lax.fori_loop(0, parts, one_part, 0)
    step = min(256, width)

    def one_column(number, carry):
        columns = pl.ds(pl.multiple_of(number * step, step), step)
        total = None
        for part in range(parts):
            both = held[part, 0:2, :, columns].reshape(2 * units, step)
            term = jnp.dot(d_ref[part], both, preferred_element_type=jnp.float32)
            total = term if total is None else total + term
        slot_ref[:, columns] = total.astype(jnp.bfloat16)
        return carry

    lax.fori_loop(0, width // step, one_column, 0)


def expert_pass(hidden_rows, weighted_rows, pieces, parts):
    count, width = hidden_rows.shape
    units = sum(piece.shape[1] for piece in pieces) // parts
    vmem = pl.BlockSpec(memory_space=pltpu.VMEM)
    return pl.pallas_call(
        functools.partial(expert_kernel, len(pieces)),
        in_specs=[vmem] * 2 + [pl.BlockSpec(memory_space=pl.ANY)] * len(pieces),
        out_specs=(vmem, vmem),
        out_shape=(
            jax.ShapeDtypeStruct((count, width), jnp.bfloat16),
            jax.ShapeDtypeStruct((parts, count, 2 * units), jnp.bfloat16),
        ),
        scratch_shapes=[
            pltpu.VMEM((parts, 3, units, width), jnp.bfloat16),
            pltpu.SemaphoreType.DMA((len(pieces),)),
        ],
        cost_estimate=pl.CostEstimate(
            flops=10 * count * width * units * parts,
            bytes_accessed=2 * width * (3 * units * parts + 3 * count),
            transcendentals=count * units * parts,
        ),
        name="expert_pass",
    )(hidden_rows, weighted_rows, *pieces)


def per_device(layer_inputs, norm_gain, w_gate, w_up, w_down, routes, probs, cotangent, sampled):
    section = lax.axis_index("section")
    upper = section == 1
    peers = lax.axis_size("expert")
    groups = lax.axis_size("mp")
    tokens, width = cotangent.shape
    top_count = routes.shape[2]

    stored = (w_gate[0], w_up[0], w_down[0])
    index = section.astype(jnp.int32).reshape(1)
    got = other_core(expert_part(1 - index, stored, 4))
    head1 = layer_part(1, 0, 2, 4, index, got, stored)
    tail1 = layer_part(1, 2, 2, 4, index, got, stored)
    head_before = turned(head1, 1)
    tail_behind = turned(tail1, -1)
    tail_before = turned(tail1, 1)
    head_behind = turned(head1, -1)
    head_far = turned(head_before, 1)
    tail_far = turned(tail_behind, -1)
    small = jnp.concatenate(
        [norm_gain[0], routes[0].astype(jnp.float32).reshape(-1), probs[0].reshape(-1)]
    )
    small_parts = lax.all_gather(small, "section", axis=0)
    input_parts = lax.all_gather(layer_inputs[0], "section", axis=0)
    own0 = layer_part(0, 0, 4, 4, index, after(got, tail1), stored)
    before0, behind0 = ring_first(after(own0, head_far, tail_far))
    far0 = turned(before0, 1)
    pieces1 = (
        head1,
        tail1,
        head_before,
        tail_before,
        head_behind,
        tail_behind,
        head_far,
        tail_far,
    )
    pieces0 = (own0, before0, behind0, far0)

    experts_here = 2 * jnp.arange(peers, dtype=jnp.int32) + section
    layers = []
    for layer in range(2):
        vector = small_parts[layer]
        gain_vector = vector[:width]
        token_routes = (
            vector[width : width + tokens * top_count].reshape(tokens, top_count).astype(jnp.int32)
        )
        token_probs = vector[width + tokens * top_count :].reshape(tokens, top_count)
        normed, factor, hidden = normalize(input_parts[layer], gain_vector)
        pick, row_prob = plan(token_routes, token_probs, experts_here)
        layers.append((gain_vector, normed, factor, hidden, pick, row_prob))

    def spread(pick, rows):
        flat = pick.astype(jnp.bfloat16).reshape(-1, pick.shape[2])
        return jnp.dot(flat, rows, preferred_element_type=jnp.float32)

    pick1, pick0 = layers[1][4], layers[0][4]

    def scaled_rows(pick, row_prob, upstream):
        rows = spread(pick, upstream) * row_prob.reshape(-1, 1)
        return rows.astype(jnp.bfloat16)

    first = jnp.concatenate(
        [
            to_wire(spread(pick1, layers[1][3]).astype(jnp.bfloat16), peers),
            to_wire(scaled_rows(pick1, layers[1][5], cotangent), peers),
        ],
        axis=1,
    )
    arrived = lax.all_to_all(first, "expert", split_axis=0, concat_axis=0, tiled=True)
    hidden1 = from_wire(arrived[:, :CAP])
    weighted1 = from_wire(arrived[:, CAP:])
    second = to_wire(spread(pick0, layers[0][3]).astype(jnp.bfloat16), peers)
    hidden0 = from_wire(lax.all_to_all(second, "expert", split_axis=0, concat_axis=0, tiled=True))
    trained1 = sampled[0] == 1

    def finish(layer, sent, upstream):
        gain_vector, normed, factor, _, pick, _ = layers[layer]
        returned = from_wire(
            lax.all_to_all(sent, "expert", split_axis=0, concat_axis=0, tiled=True)
        )
        flat = pick.astype(jnp.bfloat16).reshape(-1, tokens)
        partial = lax.dot_general(
            flat, returned, (((0,), (0,)), ((), ())), preferred_element_type=jnp.float32
        )
        token_grad = partial + other_core(partial)
        scaled = token_grad * gain_vector[None, :]
        inner = jnp.mean(scaled * normed, axis=1, keepdims=True)
        return (upstream.astype(jnp.float32) + factor * (scaled - normed * inner)).astype(
            jnp.bfloat16
        )

    slot_grad1, d_both1 = expert_pass(hidden1, weighted1, pieces1, groups)
    trained_hidden = jnp.where(trained1, *after((hidden1, hidden0), slot_grad1))
    before_h, behind_h = ring_first(after(trained_hidden, far0))
    far_h = ring_second(before_h, behind_h)
    far_h = jnp.concatenate(far_h, axis=0)
    input_grad1 = finish(1, to_wire(slot_grad1, peers), cotangent)
    weighted0 = exchange(scaled_rows(pick0, layers[0][5], input_grad1), peers)
    slot_grad0, d_both0 = expert_pass(hidden0, weighted0, pieces0, groups)
    sent0 = to_wire(slot_grad0, peers)
    input_grad0 = finish(0, sent0, input_grad1)
    result = jnp.where(upper, input_grad1, input_grad0)

    units = w_gate.shape[2]
    d_both = after(jnp.where(trained1, d_both1, d_both0), sent0)
    d_behind = turned(d_both[1], -1)
    d_before = turned(d_both[2], 1)
    d_far = turned(d_both[3], 2)
    grads = back_rows(d_both[0], trained_hidden)
    grads = grads + back_rows(d_before, before_h)
    grads = grads + back_rows(d_behind, behind_h)
    grads = grads + back_rows(d_far, far_h)
    grads = grads.astype(jnp.bfloat16)
    from_other = other_core(grads)
    trained = sampled[0] == section

    def on_owner(mine, theirs):
        low = jnp.where(upper, theirs, mine)
        high = jnp.where(upper, mine, theirs)
        pair = jnp.stack([low, high]).astype(jnp.float32)
        return jnp.where(trained, pair, 0.0)[None]

    gate_share = on_owner(grads[:units], from_other[:units])
    up_share = on_owner(grads[units:], from_other[units:])
    return (result[None], gate_share, up_share)


def solution(mesh):
    placed = (
        P("section", ("expert", "mp"), None),
        P("section", None),
        P("section", "expert", "mp", None),
        P("section", "expert", "mp", None),
        P("section", "expert", "mp", None),
        P("section", ("expert", "mp"), None),
        P("section", ("expert", "mp"), None),
        P(("expert", "mp"), None),
        P(),
    )
    return jax.shard_map(
        per_device,
        mesh=mesh,
        in_specs=placed,
        out_specs=(
            P("section", ("expert", "mp"), None),
            P("section", "expert", "mp", None),
            P("section", "expert", "mp", None),
        ),
        check_vma=False,
    )
```

```python
import functools

import jax
import jax.numpy as jnp
from jax import lax
from jax.experimental import pallas as pl
from jax.experimental.pallas import tpu as pltpu
from jax.sharding import PartitionSpec as P


CAPH = 5
CAP = 2 * CAPH
LANES = 128


epsilon = 1e-06


def other_core(value):
    return lax.ppermute(value, "section", [(0, 1), (1, 0)])


def after(value, *earlier):
    return lax.optimization_barrier((value, *earlier))[0]


def turned(value, by):
    peers = lax.axis_size("mp")
    return lax.ppermute(value, "mp", [(i, (i + by) % peers) for i in range(peers)])


def ring_first(own):
    return turned(own, 1), turned(own, -1)


def ring_second(before, behind):
    half = before.shape[-2] // 2
    return (
        turned(before[..., :half, :], 1),
        turned(behind[..., half:, :], -1),
    )


def pick_kernel(index_ref, gate_ref, up_ref, down_ref, out_ref):
    out_ref[0] = gate_ref[0]
    out_ref[1] = up_ref[0]
    out_ref[2] = down_ref[0]


def expert_part(index, weights, blocks):
    _, units, width = weights[0].shape
    rows = units // blocks
    spec = pl.BlockSpec((1, rows, width), lambda i, index_ref: (index_ref[0], i, 0))
    return pl.pallas_call(
        pick_kernel,
        grid_spec=pltpu.PrefetchScalarGridSpec(
            num_scalar_prefetch=1,
            grid=(blocks,),
            in_specs=[spec] * 3,
            out_specs=pl.BlockSpec((3, rows, width), lambda i, index_ref: (0, i, 0)),
        ),
        out_shape=jax.ShapeDtypeStruct((3, units, width), weights[0].dtype),
        name="expert_part",
    )(index, *weights)


def choose_kernel(keep, index_ref, got_ref, gate_ref, up_ref, down_ref, out_ref):
    @pl.when(index_ref[0] == keep)
    def _():
        out_ref[0] = gate_ref[0]
        out_ref[1] = up_ref[0]
        out_ref[2] = down_ref[0]

    @pl.when(index_ref[0] != keep)
    def _():
        out_ref[...] = got_ref[...]


def layer_part(layer, first, count, blocks, index, got, weights):
    _, units, width = weights[0].shape
    rows = units // blocks
    own = pl.BlockSpec((1, rows, width), lambda i, index_ref: (index_ref[0], first + i, 0))
    return pl.pallas_call(
        functools.partial(choose_kernel, layer),
        grid_spec=pltpu.PrefetchScalarGridSpec(
            num_scalar_prefetch=1,
            grid=(count,),
            in_specs=[pl.BlockSpec((3, rows, width), lambda i, index_ref: (0, first + i, 0))]
            + [own] * 3,
            out_specs=pl.BlockSpec((3, rows, width), lambda i, index_ref: (0, i, 0)),
        ),
        out_shape=jax.ShapeDtypeStruct((3, count * rows, width), weights[0].dtype),
        name="layer_part",
    )(index, got, *weights)


def normalize(inputs, gain_vector):
    values = inputs.astype(jnp.float32)
    factor = lax.rsqrt(jnp.mean(values * values, axis=1, keepdims=True) + epsilon)
    normed = values * factor
    return (normed, factor, (normed * gain_vector[None, :]).astype(jnp.bfloat16))


def plan(token_routes, token_probs, experts_here):
    match = token_routes[:, :, None] == experts_here[None, None, :]
    named = jnp.any(match, axis=1)
    chance = jnp.sum(jnp.where(match, token_probs[:, :, None], 0.0), axis=1)
    tokens = token_routes.shape[0]
    earlier = (
        jnp.arange(tokens, dtype=jnp.int32)[:, None] > jnp.arange(tokens, dtype=jnp.int32)[None, :]
    )
    places = jnp.dot(
        earlier.astype(jnp.bfloat16),
        named.astype(jnp.bfloat16),
        preferred_element_type=jnp.float32,
    ).astype(jnp.int32)
    places = jnp.where(named, places, -1).T
    pick = places[:, None, :] == jnp.arange(CAP, dtype=jnp.int32)[None, :, None]
    row_prob = jnp.sum(jnp.where(pick, chance.T[:, None, :], 0.0), axis=2)
    return pick, row_prob


def to_wire(rows, peers):
    return rows.reshape(peers, rows.shape[0] // peers, rows.shape[1] // LANES, LANES)


def from_wire(wire):
    return wire.reshape(wire.shape[0] * wire.shape[1], wire.shape[2] * wire.shape[3])


def exchange(rows, peers):
    wire = to_wire(rows, peers)
    return from_wire(lax.all_to_all(wire, "expert", split_axis=0, concat_axis=0, tiled=True))


def back_rows(weights, rows):
    return lax.dot_general(
        weights, rows, (((0,), (0,)), ((), ())), preferred_element_type=jnp.float32
    )


def expert_kernel(pieces, hidden_ref, weighted_ref, *refs):
    weight_refs, (slot_ref, d_ref, held, sems) = refs[:pieces], refs[pieces:]
    parts, _, units, width = held.shape
    start = 0
    for ref in weight_refs:
        rows = ref.shape[1]
        part, first = start // units, start % units
        there = held.at[part, :, pl.ds(first, rows), :]
        pltpu.make_async_copy(ref, there, sems.at[part]).start()
        start += rows

    def along(rows_ref, part, which):
        return lax.dot_general(
            rows_ref[...],
            held[part, which],
            (((1,), (1,)), ((), ())),
            preferred_element_type=jnp.float32,
        )

    def one_part(part, carry):
        pltpu.make_async_copy(held.at[part], held.at[part], sems.at[part]).wait()
        gate_act = along(hidden_ref, part, 0)
        lifted = along(hidden_ref, part, 1)
        back = along(weighted_ref, part, 2)
        logistic = jax.nn.sigmoid(gate_act)
        d_gate = back * lifted * logistic * (1.0 + gate_act * (1.0 - logistic))
        d_up = back * gate_act * logistic
        d_ref[part] = jnp.concatenate([d_gate, d_up], axis=1).astype(jnp.bfloat16)
        return carry

    lax.fori_loop(0, parts, one_part, 0)
    step = min(256, width)

    def one_column(number, carry):
        columns = pl.ds(pl.multiple_of(number * step, step), step)
        total = None
        for part in range(parts):
            both = held[part, 0:2, :, columns].reshape(2 * units, step)
            term = jnp.dot(d_ref[part], both, preferred_element_type=jnp.float32)
            total = term if total is None else total + term
        slot_ref[:, columns] = total.astype(jnp.bfloat16)
        return carry

    lax.fori_loop(0, width // step, one_column, 0)


def expert_pass(hidden_rows, weighted_rows, pieces, parts):
    count, width = hidden_rows.shape
    units = sum(piece.shape[1] for piece in pieces) // parts
    vmem = pl.BlockSpec(memory_space=pltpu.VMEM)
    return pl.pallas_call(
        functools.partial(expert_kernel, len(pieces)),
        in_specs=[vmem] * 2 + [pl.BlockSpec(memory_space=pl.ANY)] * len(pieces),
        out_specs=(vmem, vmem),
        out_shape=(
            jax.ShapeDtypeStruct((count, width), jnp.bfloat16),
            jax.ShapeDtypeStruct((parts, count, 2 * units), jnp.bfloat16),
        ),
        scratch_shapes=[
            pltpu.VMEM((parts, 3, units, width), jnp.bfloat16),
            pltpu.SemaphoreType.DMA((parts,)),
        ],
        cost_estimate=pl.CostEstimate(
            flops=10 * count * width * units * parts,
            bytes_accessed=2 * width * (3 * units * parts + 3 * count),
            transcendentals=count * units * parts,
        ),
        name="expert_pass",
    )(hidden_rows, weighted_rows, *pieces)


def per_device(layer_inputs, norm_gain, w_gate, w_up, w_down, routes, probs, cotangent, sampled):
    section = lax.axis_index("section")
    upper = section == 1
    peers = lax.axis_size("expert")
    groups = lax.axis_size("mp")
    tokens, width = cotangent.shape
    top_count = routes.shape[2]

    stored = (w_gate[0], w_up[0], w_down[0])
    index = section.astype(jnp.int32).reshape(1)
    got = other_core(expert_part(1 - index, stored, 4))
    head1 = layer_part(1, 0, 2, 4, index, got, stored)
    tail1 = layer_part(1, 2, 2, 4, index, got, stored)
    head_before = turned(head1, 1)
    tail_behind = turned(tail1, -1)
    tail_before = turned(tail1, 1)
    head_behind = turned(head1, -1)
    head_far = turned(head_before, 1)
    tail_far = turned(tail_behind, -1)
    small = jnp.concatenate(
        [norm_gain[0], routes[0].astype(jnp.float32).reshape(-1), probs[0].reshape(-1)]
    )
    small_parts = lax.all_gather(small, "section", axis=0)
    input_parts = lax.all_gather(layer_inputs[0], "section", axis=0)
    own0 = layer_part(0, 0, 4, 4, index, after(got, tail1), stored)
    before0, behind0 = ring_first(after(own0, head_far, tail_far))
    far0 = ring_second(before0, behind0)
    pieces1 = (
        head1,
        tail1,
        head_before,
        tail_before,
        head_behind,
        tail_behind,
        head_far,
        tail_far,
    )
    pieces0 = (own0, before0, behind0, *far0)

    experts_here = 2 * jnp.arange(peers, dtype=jnp.int32) + section
    layers = []
    for layer in range(2):
        vector = small_parts[layer]
        gain_vector = vector[:width]
        token_routes = (
            vector[width : width + tokens * top_count].reshape(tokens, top_count).astype(jnp.int32)
        )
        token_probs = vector[width + tokens * top_count :].reshape(tokens, top_count)
        normed, factor, hidden = normalize(input_parts[layer], gain_vector)
        pick, row_prob = plan(token_routes, token_probs, experts_here)
        layers.append((gain_vector, normed, factor, hidden, pick, row_prob))

    def spread(pick, rows):
        flat = pick.astype(jnp.bfloat16).reshape(-1, pick.shape[2])
        return jnp.dot(flat, rows, preferred_element_type=jnp.float32)

    pick1, pick0 = layers[1][4], layers[0][4]

    def scaled_rows(pick, row_prob, upstream):
        rows = spread(pick, upstream) * row_prob.reshape(-1, 1)
        return rows.astype(jnp.bfloat16)

    first = jnp.concatenate(
        [
            to_wire(spread(pick1, layers[1][3]).astype(jnp.bfloat16), peers),
            to_wire(scaled_rows(pick1, layers[1][5], cotangent), peers),
            to_wire(spread(pick0, layers[0][3]).astype(jnp.bfloat16), peers),
        ],
        axis=1,
    )
    arrived = lax.all_to_all(first, "expert", split_axis=0, concat_axis=0, tiled=True)
    hidden1 = from_wire(arrived[:, :CAP])
    weighted1 = from_wire(arrived[:, CAP : 2 * CAP])
    trained1 = sampled[0] == 1

    def finish(layer, sent, upstream):
        gain_vector, normed, factor, _, pick, _ = layers[layer]
        returned = from_wire(
            lax.all_to_all(sent, "expert", split_axis=0, concat_axis=0, tiled=True)
        )
        flat = pick.astype(jnp.bfloat16).reshape(-1, tokens)
        partial = lax.dot_general(
            flat, returned, (((0,), (0,)), ((), ())), preferred_element_type=jnp.float32
        )
        token_grad = partial + other_core(partial)
        scaled = token_grad * gain_vector[None, :]
        inner = jnp.mean(scaled * normed, axis=1, keepdims=True)
        return (upstream.astype(jnp.float32) + factor * (scaled - normed * inner)).astype(
            jnp.bfloat16
        )

    slot_grad1, d_both1 = expert_pass(hidden1, weighted1, pieces1, groups)
    hidden0 = from_wire(after(arrived, slot_grad1)[:, 2 * CAP :])
    trained_hidden = jnp.where(trained1, *after((hidden1, hidden0), slot_grad1))
    before_h, behind_h = ring_first(after(trained_hidden, *far0))
    far_h = ring_second(before_h, behind_h)
    far_h = jnp.concatenate(far_h, axis=0)
    input_grad1 = finish(1, to_wire(slot_grad1, peers), cotangent)
    weighted0 = exchange(scaled_rows(pick0, layers[0][5], input_grad1), peers)
    slot_grad0, d_both0 = expert_pass(hidden0, weighted0, pieces0, groups)
    sent0 = to_wire(slot_grad0, peers)
    input_grad0 = finish(0, sent0, input_grad1)
    result = jnp.where(upper, input_grad1, input_grad0)

    units = w_gate.shape[2]
    d_both = after(jnp.where(trained1, d_both1, d_both0), sent0)
    d_behind = turned(d_both[1], -1)
    d_before = turned(d_both[2], 1)
    d_far = turned(d_both[3], 2)
    grads = back_rows(d_both[0], trained_hidden)
    grads = grads + back_rows(d_before, before_h)
    grads = grads + back_rows(d_behind, behind_h)
    grads = grads + back_rows(d_far, far_h)
    grads = grads.astype(jnp.bfloat16)
    from_other = other_core(grads)
    trained = sampled[0] == section

    def on_owner(mine, theirs):
        low = jnp.where(upper, theirs, mine)
        high = jnp.where(upper, mine, theirs)
        pair = jnp.stack([low, high]).astype(jnp.float32)
        return jnp.where(trained, pair, 0.0)[None]

    gate_share = on_owner(grads[:units], from_other[:units])
    up_share = on_owner(grads[units:], from_other[units:])
    return (result[None], gate_share, up_share)


def solution(mesh):
    placed = (
        P("section", ("expert", "mp"), None),
        P("section", None),
        P("section", "expert", "mp", None),
        P("section", "expert", "mp", None),
        P("section", "expert", "mp", None),
        P("section", ("expert", "mp"), None),
        P("section", ("expert", "mp"), None),
        P(("expert", "mp"), None),
        P(),
    )
    return jax.shard_map(
        per_device,
        mesh=mesh,
        in_specs=placed,
        out_specs=(
            P("section", ("expert", "mp"), None),
            P("section", "expert", "mp", None),
            P("section", "expert", "mp", None),
        ),
        check_vma=False,
    )
```

```python
import functools

import jax
import jax.numpy as jnp
from jax import lax
from jax.experimental import pallas as pl
from jax.experimental.pallas import tpu as pltpu
from jax.sharding import PartitionSpec as P


CAPH = 5
CAP = 2 * CAPH
LANES = 128


epsilon = 1e-06


def other_core(value):
    return lax.ppermute(value, "section", [(0, 1), (1, 0)])


def after(value, *earlier):
    return lax.optimization_barrier((value, *earlier))[0]


def turned(value, by):
    peers = lax.axis_size("mp")
    return lax.ppermute(value, "mp", [(i, (i + by) % peers) for i in range(peers)])


def ring_first(own):
    return turned(own, 1), turned(own, -1)


def ring_second(before, behind):
    half = before.shape[-2] // 2
    return (
        turned(before[..., :half, :], 1),
        turned(behind[..., half:, :], -1),
    )


def pick_kernel(index_ref, gate_ref, up_ref, down_ref, out_ref):
    out_ref[0] = gate_ref[0]
    out_ref[1] = up_ref[0]
    out_ref[2] = down_ref[0]


def expert_part(index, weights, blocks):
    _, units, width = weights[0].shape
    rows = units // blocks
    spec = pl.BlockSpec((1, rows, width), lambda i, index_ref: (index_ref[0], i, 0))
    return pl.pallas_call(
        pick_kernel,
        grid_spec=pltpu.PrefetchScalarGridSpec(
            num_scalar_prefetch=1,
            grid=(blocks,),
            in_specs=[spec] * 3,
            out_specs=pl.BlockSpec((3, rows, width), lambda i, index_ref: (0, i, 0)),
        ),
        out_shape=jax.ShapeDtypeStruct((3, units, width), weights[0].dtype),
        name="expert_part",
    )(index, *weights)


def choose_kernel(keep, index_ref, got_ref, gate_ref, up_ref, down_ref, out_ref):
    @pl.when(index_ref[0] == keep)
    def _():
        out_ref[0] = gate_ref[0]
        out_ref[1] = up_ref[0]
        out_ref[2] = down_ref[0]

    @pl.when(index_ref[0] != keep)
    def _():
        out_ref[...] = got_ref[...]


def layer_part(layer, first, count, blocks, index, got, weights):
    _, units, width = weights[0].shape
    rows = units // blocks
    own = pl.BlockSpec((1, rows, width), lambda i, index_ref: (index_ref[0], first + i, 0))
    return pl.pallas_call(
        functools.partial(choose_kernel, layer),
        grid_spec=pltpu.PrefetchScalarGridSpec(
            num_scalar_prefetch=1,
            grid=(count,),
            in_specs=[pl.BlockSpec((3, rows, width), lambda i, index_ref: (0, first + i, 0))]
            + [own] * 3,
            out_specs=pl.BlockSpec((3, rows, width), lambda i, index_ref: (0, i, 0)),
        ),
        out_shape=jax.ShapeDtypeStruct((3, count * rows, width), weights[0].dtype),
        name="layer_part",
    )(index, got, *weights)


def deliver_kernel(flags_ref, mine_ref, theirs_ref, gate_ref, up_ref):
    units = gate_ref.shape[2]
    own = flags_ref[0] == pl.program_id(0)
    trained = flags_ref[1] == 1

    def fill(part_ref):
        gate_ref[0, 0] = part_ref[:units].astype(jnp.float32)
        up_ref[0, 0] = part_ref[units:].astype(jnp.float32)

    @pl.when(jnp.logical_and(trained, own))
    def _():
        fill(mine_ref)

    @pl.when(jnp.logical_and(trained, jnp.logical_not(own)))
    def _():
        fill(theirs_ref)

    @pl.when(jnp.logical_not(trained))
    def _():
        gate_ref[...] = jnp.zeros_like(gate_ref)
        up_ref[...] = jnp.zeros_like(up_ref)


def deliver(section, trained, mine, theirs):
    both, width = mine.shape
    flags = jnp.stack([section.astype(jnp.int32), trained.astype(jnp.int32)])
    whole = pl.BlockSpec((both, width), lambda i, flags_ref: (0, 0))
    one = pl.BlockSpec((1, 1, both // 2, width), lambda i, flags_ref: (0, i, 0, 0))
    shape = jax.ShapeDtypeStruct((1, 2, both // 2, width), jnp.float32)
    return pl.pallas_call(
        deliver_kernel,
        grid_spec=pltpu.PrefetchScalarGridSpec(
            num_scalar_prefetch=1,
            grid=(2,),
            in_specs=[whole, whole],
            out_specs=(one, one),
        ),
        out_shape=(shape, shape),
        name="deliver",
    )(flags, mine, theirs)


def normalize(inputs, gain_vector):
    values = inputs.astype(jnp.float32)
    factor = lax.rsqrt(jnp.mean(values * values, axis=1, keepdims=True) + epsilon)
    normed = values * factor
    return (normed, factor, (normed * gain_vector[None, :]).astype(jnp.bfloat16))


def plan(token_routes, token_probs, experts_here):
    match = token_routes[:, :, None] == experts_here[None, None, :]
    named = jnp.any(match, axis=1)
    chance = jnp.sum(jnp.where(match, token_probs[:, :, None], 0.0), axis=1)
    tokens = token_routes.shape[0]
    earlier = (
        jnp.arange(tokens, dtype=jnp.int32)[:, None] > jnp.arange(tokens, dtype=jnp.int32)[None, :]
    )
    places = jnp.dot(
        earlier.astype(jnp.bfloat16),
        named.astype(jnp.bfloat16),
        preferred_element_type=jnp.float32,
    ).astype(jnp.int32)
    places = jnp.where(named, places, -1).T
    pick = places[:, None, :] == jnp.arange(CAP, dtype=jnp.int32)[None, :, None]
    row_prob = jnp.sum(jnp.where(pick, chance.T[:, None, :], 0.0), axis=2)
    return pick, row_prob


def to_wire(rows, peers):
    return rows.reshape(peers, rows.shape[0] // peers, rows.shape[1] // LANES, LANES)


def from_wire(wire):
    return wire.reshape(wire.shape[0] * wire.shape[1], wire.shape[2] * wire.shape[3])


def exchange(rows, peers):
    wire = to_wire(rows, peers)
    return from_wire(lax.all_to_all(wire, "expert", split_axis=0, concat_axis=0, tiled=True))


def back_rows(weights, rows):
    return lax.dot_general(
        weights, rows, (((0,), (0,)), ((), ())), preferred_element_type=jnp.float32
    )


def expert_kernel(pieces, hidden_ref, weighted_ref, *refs):
    weight_refs, (slot_ref, d_ref, held, sems) = refs[:pieces], refs[pieces:]
    parts, _, units, width = held.shape
    start = 0
    for ref in weight_refs:
        rows = ref.shape[1]
        part, first = start // units, start % units
        there = held.at[part, :, pl.ds(first, rows), :]
        pltpu.make_async_copy(ref, there, sems.at[part]).start()
        start += rows

    def along(rows_ref, part, which):
        return lax.dot_general(
            rows_ref[...],
            held[part, which],
            (((1,), (1,)), ((), ())),
            preferred_element_type=jnp.float32,
        )

    def one_part(part, carry):
        pltpu.make_async_copy(held.at[part], held.at[part], sems.at[part]).wait()
        gate_act = along(hidden_ref, part, 0)
        lifted = along(hidden_ref, part, 1)
        back = along(weighted_ref, part, 2)
        logistic = jax.nn.sigmoid(gate_act)
        d_gate = back * lifted * logistic * (1.0 + gate_act * (1.0 - logistic))
        d_up = back * gate_act * logistic
        d_ref[part] = jnp.concatenate([d_gate, d_up], axis=1).astype(jnp.bfloat16)
        return carry

    lax.fori_loop(0, parts, one_part, 0)
    step = min(256, width)

    def one_column(number, carry):
        columns = pl.ds(pl.multiple_of(number * step, step), step)
        total = None
        for part in range(parts):
            both = held[part, 0:2, :, columns].reshape(2 * units, step)
            term = jnp.dot(d_ref[part], both, preferred_element_type=jnp.float32)
            total = term if total is None else total + term
        slot_ref[:, columns] = total.astype(jnp.bfloat16)
        return carry

    lax.fori_loop(0, width // step, one_column, 0)


def expert_pass(hidden_rows, weighted_rows, pieces, parts):
    count, width = hidden_rows.shape
    units = sum(piece.shape[1] for piece in pieces) // parts
    vmem = pl.BlockSpec(memory_space=pltpu.VMEM)
    return pl.pallas_call(
        functools.partial(expert_kernel, len(pieces)),
        in_specs=[vmem] * 2 + [pl.BlockSpec(memory_space=pl.ANY)] * len(pieces),
        out_specs=(vmem, vmem),
        out_shape=(
            jax.ShapeDtypeStruct((count, width), jnp.bfloat16),
            jax.ShapeDtypeStruct((parts, count, 2 * units), jnp.bfloat16),
        ),
        scratch_shapes=[
            pltpu.VMEM((parts, 3, units, width), jnp.bfloat16),
            pltpu.SemaphoreType.DMA((parts,)),
        ],
        cost_estimate=pl.CostEstimate(
            flops=10 * count * width * units * parts,
            bytes_accessed=2 * width * (3 * units * parts + 3 * count),
            transcendentals=count * units * parts,
        ),
        name="expert_pass",
    )(hidden_rows, weighted_rows, *pieces)


def per_device(layer_inputs, norm_gain, w_gate, w_up, w_down, routes, probs, cotangent, sampled):
    section = lax.axis_index("section")
    upper = section == 1
    peers = lax.axis_size("expert")
    groups = lax.axis_size("mp")
    tokens, width = cotangent.shape
    top_count = routes.shape[2]

    stored = (w_gate[0], w_up[0], w_down[0])
    small = jnp.concatenate(
        [norm_gain[0], routes[0].astype(jnp.float32).reshape(-1), probs[0].reshape(-1)]
    )
    small_parts = lax.all_gather(small, "section", axis=0)
    input_parts = lax.all_gather(layer_inputs[0], "section", axis=0)
    index = after(section.astype(jnp.int32).reshape(1), small_parts, input_parts)
    got = other_core(expert_part(1 - index, stored, 4))
    head1 = layer_part(1, 0, 2, 4, index, got, stored)
    tail1 = layer_part(1, 2, 2, 4, index, got, stored)
    head_before = turned(head1, 1)
    tail_behind = turned(tail1, -1)
    tail_before = turned(tail1, 1)
    head_behind = turned(head1, -1)
    head_far = turned(head_before, 1)
    tail_far = turned(tail_behind, -1)
    own0 = layer_part(0, 0, 4, 4, index, after(got, tail1), stored)
    before0, behind0 = ring_first(after(own0, head_far, tail_far))
    far0 = ring_second(before0, behind0)
    pieces1 = (
        head1,
        tail1,
        head_before,
        tail_before,
        head_behind,
        tail_behind,
        head_far,
        tail_far,
    )
    pieces0 = (own0, before0, behind0, *far0)

    experts_here = 2 * jnp.arange(peers, dtype=jnp.int32) + section
    layers = []
    for layer in range(2):
        vector = small_parts[layer]
        gain_vector = vector[:width]
        token_routes = (
            vector[width : width + tokens * top_count].reshape(tokens, top_count).astype(jnp.int32)
        )
        token_probs = vector[width + tokens * top_count :].reshape(tokens, top_count)
        normed, factor, hidden = normalize(input_parts[layer], gain_vector)
        pick, row_prob = plan(token_routes, token_probs, experts_here)
        layers.append((gain_vector, normed, factor, hidden, pick, row_prob))

    def spread(pick, rows):
        flat = pick.astype(jnp.bfloat16).reshape(-1, pick.shape[2])
        return jnp.dot(flat, rows, preferred_element_type=jnp.float32)

    pick1, pick0 = layers[1][4], layers[0][4]

    def scaled_rows(pick, row_prob, upstream):
        rows = spread(pick, upstream) * row_prob.reshape(-1, 1)
        return rows.astype(jnp.bfloat16)

    first = jnp.concatenate(
        [
            to_wire(spread(pick1, layers[1][3]).astype(jnp.bfloat16), peers),
            to_wire(scaled_rows(pick1, layers[1][5], cotangent), peers),
            to_wire(spread(pick0, layers[0][3]).astype(jnp.bfloat16), peers),
        ],
        axis=1,
    )
    arrived = lax.all_to_all(first, "expert", split_axis=0, concat_axis=0, tiled=True)
    hidden1 = from_wire(arrived[:, :CAP])
    weighted1 = from_wire(arrived[:, CAP : 2 * CAP])
    trained1 = sampled[0] == 1

    def finish(layer, sent, upstream):
        gain_vector, normed, factor, _, pick, _ = layers[layer]
        returned = from_wire(
            lax.all_to_all(sent, "expert", split_axis=0, concat_axis=0, tiled=True)
        )
        flat = pick.astype(jnp.bfloat16).reshape(-1, tokens)
        partial = lax.dot_general(
            flat, returned, (((0,), (0,)), ((), ())), preferred_element_type=jnp.float32
        )
        token_grad = partial + other_core(partial)
        scaled = token_grad * gain_vector[None, :]
        inner = jnp.mean(scaled * normed, axis=1, keepdims=True)
        return (upstream.astype(jnp.float32) + factor * (scaled - normed * inner)).astype(
            jnp.bfloat16
        )

    slot_grad1, d_both1 = expert_pass(hidden1, weighted1, pieces1, groups)
    hidden0 = from_wire(after(arrived, slot_grad1)[:, 2 * CAP :])
    trained_hidden = jnp.where(trained1, *after((hidden1, hidden0), slot_grad1))
    before_h, behind_h = ring_first(after(trained_hidden, *far0))
    far_h = ring_second(before_h, behind_h)
    far_h = jnp.concatenate(far_h, axis=0)
    input_grad1 = finish(1, to_wire(slot_grad1, peers), cotangent)
    weighted0 = exchange(scaled_rows(pick0, layers[0][5], input_grad1), peers)
    slot_grad0, d_both0 = expert_pass(hidden0, weighted0, pieces0, groups)
    sent0 = to_wire(slot_grad0, peers)
    input_grad0 = finish(0, sent0, input_grad1)
    result = jnp.where(upper, input_grad1, input_grad0)

    d_both = after(jnp.where(trained1, d_both1, d_both0), sent0)
    d_behind = turned(d_both[1], -1)
    d_before = turned(d_both[2], 1)
    d_far = turned(d_both[3], 2)
    grads = back_rows(d_both[0], trained_hidden)
    grads = grads + back_rows(d_before, before_h)
    grads = grads + back_rows(d_behind, behind_h)
    grads = grads + back_rows(d_far, far_h)
    grads = grads.astype(jnp.bfloat16)
    from_other = other_core(grads)
    trained = sampled[0] == section

    gate_share, up_share = deliver(section, trained, grads, from_other)
    return (result[None], gate_share, up_share)


def solution(mesh):
    placed = (
        P("section", ("expert", "mp"), None),
        P("section", None),
        P("section", "expert", "mp", None),
        P("section", "expert", "mp", None),
        P("section", "expert", "mp", None),
        P("section", ("expert", "mp"), None),
        P("section", ("expert", "mp"), None),
        P(("expert", "mp"), None),
        P(),
    )
    return jax.shard_map(
        per_device,
        mesh=mesh,
        in_specs=placed,
        out_specs=(
            P("section", ("expert", "mp"), None),
            P("section", "expert", "mp", None),
            P("section", "expert", "mp", None),
        ),
        check_vma=False,
    )
```
